512 devices in a mesh: row: 32 (over x, y_lo, core), col: 16 (over z, y_hi).
Axes of the slice: x: 4, y: 8 (y_hi: 2, y_lo: 4; y = y_hi * 4 + y_lo), z: 8, core: 2. Of those that a mesh axis runs over, the one named last changes fastest.
Arguments:
- legendre: bfloat16 [4, 128, 23, 32, 128], P(None, 'col', None, 'row'), may hold values from -6 to 6
- longitude: float32 [512], replicated, may hold values from -3.140625 to 3.140625
- obs_weight: float32 [512], replicated, may hold values from 0.1 to 1.9
- span_weight: float32 [8], replicated, may hold values from 0.3 to 3
- span_of: int32 [512], replicated, may hold values from 0 to 7
- tile_order: int32 [736], replicated, may hold values from 0 to 735, each once
- slab_start: int32 [1], replicated, may hold values from 0 to 692
- resident: float32 [23, 32, 16, 128, 128], P(None, 'row', 'col'), may hold values from -6 to 6
Outputs:
- updated: float32 [23, 32, 16, 128, 128], P(None, 'row', 'col')
The draws below stay inside these ranges and needn't reach their ends.
Inputs may be any that keep to these rules, and one draw needn't show every extreme that they name: tile_order is a permutation of the slot positions.
All inputs are finite; a program needn't handle non-finite values.
Results may differ from the reference program's by a relative error of at most 0.00074.
Values may be sent and summed in bfloat16 or wider, within the bound.
A program may use at most 64 MiB of HBM per device.

```python
import math
import jax
import jax.numpy as jnp
from jax import lax

DEGREE = 300
UNK = 90600
TILE = 128
SPAN = 128
BLOCKS = 4
GROUPS = 8
OBS = 512
TILES = 708
ROW_SLOTS = 23
TILES_PAD = 736
N_ROW = 32
N_COL = 16


def with_ends(values, own_key, low, high):
    spot = [jax.random.randint(jax.random.fold_in(own_key, axis), (), 0, length) for axis, length in enumerate(values.shape)]
    widest = values.shape.index(max(values.shape))
    neighbour = spot[:widest] + [(spot[widest] + 1) % values.shape[widest]] + spot[widest + 1:]
    return values.at[tuple(spot)].set(low).at[tuple(neighbour)].set(high)


def block_scale(stream_key, dims, cuts, least, largest):
    def one(position, shards_of):
        draws = jax.random.uniform(jax.random.fold_in(jax.random.fold_in(stream_key, 6), position), (shards_of,), jnp.float32, least / len(cuts), largest / len(cuts))
        return jnp.repeat(jnp.exp(draws), dims[position] // shards_of).reshape((-1,) + (1,) * (len(dims) - position - 1))

    factor_of = one(*cuts[0])
    for cut in cuts[1:]:
        factor_of = factor_of * one(*cut)
    return factor_of


def gaussian(own_key, dims, scale, bound, split=(), kind=jnp.bfloat16):
    entries = jax.random.normal(own_key, dims, jnp.float32) * scale
    if len(split) > 0:
        entries = block_scale(own_key, dims, split, -0.22, 0.18) * entries
    return jnp.clip(entries, min=-bound, max=bound).astype(kind)


def setup_inputs(seed: int = 0) -> dict:
    key_list = jax.random.split(jax.random.key(seed), 9)
    return {
        "legendre": gaussian(key_list[0], (BLOCKS, SPAN, ROW_SLOTS, N_ROW, TILE), 1.0, 6.0, ((1, 16), (3, 32))),
        "longitude": jnp.clip(jax.random.uniform(key_list[1], (OBS,), jnp.float32, -3.140625, 3.140625), -3.140625, 3.140625),
        "obs_weight": jnp.clip(1.0 + 0.18 * jax.random.normal(key_list[2], (OBS,), jnp.float32), 0.1, 1.9),
        "span_weight": jnp.clip(jnp.exp(jax.random.uniform(key_list[3], (GROUPS,), jnp.float32, math.log(0.3), math.log(3.0))), 0.3, 3.0),
        "span_of": with_ends(jax.random.randint(key_list[4], (OBS,), 0, GROUPS), jax.random.fold_in(key_list[4], 1), 0, GROUPS - 1).astype(jnp.int32),
        "tile_order": jax.random.permutation(key_list[5], TILES_PAD).astype(jnp.int32),
        "slab_start": jax.random.randint(key_list[6], (1,), 0, TILES - N_COL + 1).astype(jnp.int32),
        "resident": gaussian(key_list[7], (ROW_SLOTS, N_ROW, N_COL, TILE, TILE), 1.0, 6.0, ((1, 32), (2, 16)), jnp.float32),
    }


def reference(legendre, longitude, obs_weight, span_weight, span_of, tile_order, slab_start, resident):
    slot_total = ROW_SLOTS * N_ROW
    unknown = tile_order[:, None] * TILE + jnp.arange(TILE, dtype=jnp.int32)[None, :]
    orders = (unknown % (DEGREE + 1)).astype(jnp.float32).reshape(1, slot_total * TILE)
    is_valid = (unknown < UNK).reshape(1, slot_total * TILE)
    values = legendre.reshape(OBS, slot_total * TILE).astype(jnp.float32)
    design = jnp.where(is_valid, values * jnp.cos(longitude[:, None] * orders), 0.0).astype(jnp.bfloat16)
    matches = span_of[:, None] == jnp.arange(GROUPS, dtype=jnp.int32)[None, :]
    factor = lax.optimization_barrier(jnp.sum(jnp.where(matches, span_weight[None, :], 0.0), axis=1))
    weight = obs_weight * factor * (0.25 / math.sqrt(OBS))
    targets = slab_start[0] + jnp.arange(N_COL, dtype=jnp.int32)
    places = jnp.arange(slot_total, dtype=jnp.int32)
    positions = lax.optimization_barrier(jnp.sum(jnp.where(tile_order[None, :] == targets[:, None], places[None, :], 0), axis=1)).astype(jnp.int32)
    columns = design.reshape(OBS, slot_total, TILE)[:, positions, :]
    weighted = (weight[:, None, None] * columns.astype(jnp.float32)).astype(jnp.bfloat16)
    products = lax.dot_general(design.astype(jnp.float32), weighted.reshape(OBS, N_COL * TILE).astype(jnp.float32), (((0,), (0,)), ((), ())), precision=lax.Precision.HIGHEST, preferred_element_type=jnp.float32)
    products = products.reshape(ROW_SLOTS, N_ROW, TILE, N_COL, TILE).transpose(0, 1, 3, 2, 4)
    in_lower = tile_order.reshape(ROW_SLOTS, N_ROW)[:, :, None] >= targets[None, None, :]
    return resident + jnp.where(in_lower[:, :, :, None, None], products, 0.0)
```

```python
import functools
import math

import jax
import jax.numpy as jnp
from jax import lax
from jax.experimental import pallas as pl
from jax.experimental.pallas import tpu as pltpu
from jax.sharding import Mesh
from jax.sharding import PartitionSpec as P

DEGREE = 300
UNK = 90600
MESH = pl.DeviceIdType.MESH
NX, NYL, NCORE, NZ, NYH = 4, 4, 2, 8, 2
NROW = NX * NYL * NCORE
NCOL = NZ * NYH
SLOTS = 23
TILE = 128
OBS = 512
SHARD = OBS // NCOL
CHUNKS = ((0, 6), (6, 6), (12, 6), (18, 5))


def ring_hops(chunk):
    return (4, 3) if chunk % 2 == 0 else (3, 4)


def kernel(
    leg,
    lon,
    obs_w,
    span_w,
    span_of,
    order,
    slab,
    prod,
    table,
    own,
    gath,
    pair,
    sendy,
    masked,
    parts,
    column,
    weighted,
    wcol,
    ring_send,
    ring_recv,
    y_send,
    y_recv,
    c_send,
    c_recv,
):
    x, yl, core = lax.axis_index("x"), lax.axis_index("yl"), lax.axis_index("core")
    z, yh = lax.axis_index("z"), lax.axis_index("yh")
    row = (x * NYL + yl) * NCORE + core
    mine = z * NYH + yh
    other = 1 - yh

    def row_id(k):
        return {"x": k // (NYL * NCORE), "yl": (k // NCORE) % NYL, "core": k % NCORE}

    barrier = pltpu.get_barrier_semaphore()

    def hello_row(i, c):
        pl.semaphore_signal(barrier, inc=1, device_id=row_id((row + i) % NROW), device_id_type=MESH)
        return c

    def hello_z(i, c):
        pl.semaphore_signal(barrier, inc=1, device_id={"z": (z + i) % NZ}, device_id_type=MESH)
        return c

    pl.semaphore_signal(barrier, inc=1, device_id={"yh": other}, device_id_type=MESH)
    lax.fori_loop(1, NZ, hello_z, 0)
    lax.fori_loop(1, NROW, hello_row, 0)

    sub = lax.broadcasted_iota(jnp.int32, (8, TILE), 0)
    lane = lax.broadcasted_iota(jnp.int32, (8, TILE), 1)
    for b in range(4):
        own_lon = jnp.zeros((8, TILE), jnp.float32)
        for j in range(8):
            own_lon = jnp.where(sub == j, lon[b * TILE + mine * 8 + j], own_lon)
        for a in range(4):
            k = lane + a * TILE
            m = jnp.where(k > DEGREE, k - (DEGREE + 1), k).astype(jnp.float32)
            table[a, pl.ds(b * 8, 8), :] = jnp.cos(own_lon * m)

    lane32 = lax.broadcasted_iota(jnp.int32, (SHARD, TILE), 1)
    tiles = []
    for s in range(SLOTS):
        t = order[s * NROW + row]
        tiles.append(t)
        whole = (t * 111477) >> 18
        start = t * TILE - whole * (DEGREE + 1)
        a0 = start // TILE
        shift = start - a0 * TILE
        back = (TILE - shift) % TILE
        low = pltpu.roll(table[a0], back, 1)
        high = pltpu.roll(table[a0 + 1], back, 1)
        cosine = jnp.where(lane32 < TILE - shift, low, high)
        values = jnp.concatenate([leg[b, s].astype(jnp.float32) for b in range(4)], axis=0)
        value = jnp.where(lane32 < UNK - t * TILE, values * cosine, 0.0)
        own[s] = value.astype(jnp.bfloat16)
        gath[mine, s] = own[s]

    base = slab[0]
    for q in range(NCOL):
        at = jnp.int32(0)
        found = jnp.int32(0)
        for s in range(SLOTS):
            hit = tiles[s] == base + q
            at = jnp.where(hit, s, at)
            found = jnp.where(hit, 1, found)
        got = own[at].astype(jnp.float32)
        got = jnp.where(found == 1, got, 0.0).astype(jnp.bfloat16)
        cand = got.reshape(2, 16, TILE)
        zq, yq = q // NYH, q % NYH
        sendy[yq, zq] = cand

    pl.semaphore_wait(barrier, 1 + (NZ - 1) + (NROW - 1))

    def ring(direction, which, hop, chunk):
        s0, n = CHUNKS[chunk]
        sign = 1 if direction == 0 else -1
        src_z = (z - sign * (hop - 1) + NZ) % NZ
        src_y = yh if which == 0 else other
        ref = gath.at[src_z * NYH + src_y, pl.ds(s0, n)]
        return pltpu.make_async_remote_copy(
            src_ref=own.at[pl.ds(s0, n)] if which == 0 and hop == 1 else ref,
            dst_ref=ref,
            send_sem=ring_send.at[direction, which, hop - 1, chunk],
            recv_sem=ring_recv.at[direction, which, hop - 1, chunk],
            device_id={"z": (z + sign + NZ) % NZ},
            device_id_type=MESH,
        )

    def ring_arrival(direction, which, hop, chunk):
        s0, n = CHUNKS[chunk]
        sign = 1 if direction == 0 else -1
        src_z = (z - sign * hop + NZ) % NZ
        src_y = yh if which == 0 else other
        ref = gath.at[src_z * NYH + src_y, pl.ds(s0, n)]
        return pltpu.make_async_remote_copy(
            src_ref=ref,
            dst_ref=ref,
            send_sem=ring_send.at[direction, which, hop - 1, chunk],
            recv_sem=ring_recv.at[direction, which, hop - 1, chunk],
            device_id={"z": (z + sign + NZ) % NZ},
            device_id_type=MESH,
        )

    started = []

    def go(copy):
        copy.start()
        started.append(copy)

    def across(chunk):
        s0, n = CHUNKS[chunk]
        return pltpu.make_async_remote_copy(
            src_ref=own.at[pl.ds(s0, n)],
            dst_ref=gath.at[mine, pl.ds(s0, n)],
            send_sem=y_send.at[chunk],
            recv_sem=y_recv.at[chunk],
            device_id={"yh": other},
            device_id_type=MESH,
        )

    def across_arrival(chunk):
        s0, n = CHUNKS[chunk]
        ref = gath.at[z * NYH + other, pl.ds(s0, n)]
        return pltpu.make_async_remote_copy(
            src_ref=ref,
            dst_ref=ref,
            send_sem=y_send.at[chunk],
            recv_sem=y_recv.at[chunk],
            device_id={"yh": other},
            device_id_type=MESH,
        )

    chunks = range(len(CHUNKS))
    swap = pltpu.make_async_remote_copy(
        src_ref=sendy.at[other],
        dst_ref=pair,
        send_sem=c_send.at[0],
        recv_sem=c_recv.at[0],
        device_id={"yh": other},
        device_id_type=MESH,
    )
    go(swap)
    for g in chunks:
        go(ring(0, 0, 1, g))
        go(ring(1, 0, 1, g))
        go(across(g))

    def ring_round(which, hop):
        for g in chunks:
            for direction in (0, 1):
                last = ring_hops(g)[direction]
                if hop <= last:
                    ring_arrival(direction, which, hop, g).wait_recv()
                if hop < last:
                    go(ring(direction, which, hop + 1, g))

    ring_round(0, 1)

    swap_in = pltpu.make_async_remote_copy(
        src_ref=sendy.at[other],
        dst_ref=pair,
        send_sem=c_send.at[0],
        recv_sem=c_recv.at[0],
        device_id={"yh": other},
        device_id_type=MESH,
    )
    swap_in.wait_recv()

    def z_send(i, c):
        peer = (z + i) % NZ
        for half, source in ((yh, sendy.at[yh, peer]), (other, pair.at[peer])):
            pltpu.make_async_remote_copy(
                src_ref=source,
                dst_ref=masked.at[pl.ds((z * NYH + half) * 2, 2)],
                send_sem=c_send.at[1],
                recv_sem=c_recv.at[1],
                device_id={"z": peer},
                device_id_type=MESH,
            ).start()
        return c

    lax.fori_loop(1, NZ, z_send, 0)
    masked[pl.ds((z * NYH + yh) * 2, 2)] = sendy[yh, z]
    masked[pl.ds((z * NYH + other) * 2, 2)] = pair[z]

    ring_round(0, 2)

    z_bytes = masked.at[pl.ds(0, 4 * (NZ - 1))]
    pltpu.make_async_copy(z_bytes, z_bytes, c_recv.at[1]).wait()
    pltpu.make_async_copy(z_bytes, z_bytes, c_send.at[1]).wait()

    def scatter(i, c):
        k = (row + i) % NROW
        pltpu.make_async_remote_copy(
            src_ref=masked.at[k],
            dst_ref=parts.at[row],
            send_sem=c_send.at[2],
            recv_sem=c_recv.at[2],
            device_id=row_id(k),
            device_id_type=MESH,
        ).start()
        return c

    lax.fori_loop(1, NROW, scatter, 0)
    parts[row] = masked[row]

    weights = jnp.zeros((4, TILE), jnp.float32)
    for g in range(8):
        weights = jnp.where(span_of[...] == g, span_w[g], weights)
    weights = obs_w[...] * weights * (0.25 / math.sqrt(OBS))
    for b in range(4):
        wide = jnp.broadcast_to(weights[b : b + 1, :], (TILE, TILE))
        wcol[:, b] = jnp.transpose(wide).reshape(NCOL, 8, TILE)

    ring_round(0, 3)

    p_bytes = parts.at[pl.ds(0, NROW - 1)]
    pltpu.make_async_copy(p_bytes, p_bytes, c_recv.at[2]).wait()
    pltpu.make_async_copy(p_bytes, p_bytes, c_send.at[2]).wait()
    total = parts[0].astype(jnp.float32)
    for k in range(1, NROW):
        total = total + parts[k].astype(jnp.float32)
    column[row] = total.astype(jnp.bfloat16)

    for g in chunks:
        across_arrival(g).wait_recv()
        go(ring(0, 1, 1, g))
        go(ring(1, 1, 1, g))

    def spread(i, c):
        k = (row + i) % NROW
        pltpu.make_async_remote_copy(
            src_ref=column.at[row],
            dst_ref=column.at[row],
            send_sem=c_send.at[3],
            recv_sem=c_recv.at[3],
            device_id=row_id(k),
            device_id_type=MESH,
        ).start()
        return c

    lax.fori_loop(1, NROW, spread, 0)

    ring_round(0, 4)
    ring_round(1, 1)
    ring_round(1, 2)

    a_bytes = column.at[pl.ds(0, NROW - 1)]
    pltpu.make_async_copy(a_bytes, a_bytes, c_recv.at[3]).wait()
    pltpu.make_async_copy(a_bytes, a_bytes, c_send.at[3]).wait()
    for c in range(NCOL):
        col = column[pl.ds(2 * c, 2)].reshape(SHARD, TILE).astype(jnp.float32)
        weighted[pl.ds(c * SHARD, SHARD)] = (col * wcol[c].reshape(SHARD, TILE)).astype(jnp.bfloat16)

    ring_round(1, 3)

    target = base + mine
    for g in chunks:
        direction = 0 if ring_hops(g)[0] == 4 else 1
        ring_arrival(direction, 1, 4, g).wait_recv()
        s0, n = CHUNKS[g]
        for s in range(s0, s0 + n):
            left = gath[:, s].reshape(OBS, TILE)
            product = lax.dot_general(
                left, weighted[...], (((0,), (0,)), ((), ())), preferred_element_type=jnp.float32
            )
            prod[s] = jnp.where(tiles[s] >= target, product, 0.0)
    for copy in started:
        copy.wait_send()


def per_device(
    legendre, longitude, obs_weight, span_weight, span_of, tile_order, slab_start, resident
):
    leg = legendre.reshape(4, 8, SLOTS, TILE).transpose(0, 2, 1, 3)
    smem = pl.BlockSpec(memory_space=pltpu.SMEM)
    vmem = pl.BlockSpec(memory_space=pltpu.VMEM)
    bf16, f32 = jnp.bfloat16, jnp.float32
    dma = pltpu.SemaphoreType.DMA
    product = pl.pallas_call(
        kernel,
        out_shape=jax.ShapeDtypeStruct((SLOTS, TILE, TILE), f32),
        in_specs=[vmem, smem, vmem, smem, vmem, smem, smem],
        out_specs=vmem,
        scratch_shapes=[
            pltpu.VMEM((4, SHARD, TILE), f32),
            pltpu.VMEM((SLOTS, SHARD, TILE), bf16),
            pltpu.VMEM((NCOL, SLOTS, SHARD, TILE), bf16),
            pltpu.VMEM((NZ, 2, 16, TILE), bf16),
            pltpu.VMEM((NYH, NZ, 2, 16, TILE), bf16),
            pltpu.VMEM((NROW, 16, TILE), bf16),
            pltpu.VMEM((NROW, 16, TILE), bf16),
            pltpu.VMEM((NROW, 16, TILE), bf16),
            pltpu.VMEM((OBS, TILE), bf16),
            pltpu.VMEM((NCOL, 4, 8, TILE), f32),
            dma((2, 2, 4, len(CHUNKS))),
            dma((2, 2, 4, len(CHUNKS))),
            dma((len(CHUNKS),)),
            dma((len(CHUNKS),)),
            dma((4,)),
            dma((4,)),
        ],
        compiler_params=pltpu.CompilerParams(
            collective_id=0, has_side_effects=True, vmem_limit_bytes=24 * 1024 * 1024
        ),
    )(
        leg,
        longitude,
        obs_weight.reshape(4, TILE),
        span_weight,
        span_of.reshape(4, TILE),
        tile_order,
        slab_start,
    )
    return resident + product.reshape(resident.shape)


def solution(mesh):
    torus = Mesh(
        mesh.devices.reshape(NX, NYL, NCORE, NZ, NYH), ("x", "yl", "core", "z", "yh")
    )
    rows, cols = ("x", "yl", "core"), ("z", "yh")
    return jax.shard_map(
        per_device,
        mesh=torus,
        in_specs=(
            P(None, cols, None, rows, None),
            P(),
            P(),
            P(),
            P(),
            P(),
            P(),
            P(None, rows, cols, None, None),
        ),
        out_specs=P(None, rows, cols, None, None),
        check_vma=False,
    )
```

```python
import functools
import math

import jax
import jax.numpy as jnp
from jax import lax
from jax.experimental import pallas as pl
from jax.experimental.pallas import tpu as pltpu
from jax.sharding import Mesh
from jax.sharding import PartitionSpec as P

DEGREE = 300
UNK = 90600
TILES = 708
MESH = pl.DeviceIdType.MESH
NX, NYL, NCORE, NZ, NYH = 4, 4, 2, 8, 2
NROW = NX * NYL * NCORE
NCOL = NZ * NYH
SLOTS = 23
TILE = 128
OBS = 512
SHARD = OBS // NCOL
SIZES = (10, 14, 17, 20, 23)


def chunks_of(slots):
    count = min(4, slots)
    edges = [slots * i // count for i in range(count + 1)]
    return tuple((a, b - a) for a, b in zip(edges[:-1], edges[1:]))


def hops(which, chunk):
    if which == 1:
        return (3, 3)
    return (4, 3) if chunk % 2 == 0 else (3, 4)


def plan_of(slots):
    if slots > 14:
        return (
            (0, 1), (0, 2), "added", (0, 3), "others", (0, 4), "spread", (1, 1), (1, 2), "in",
        )
    return (
        (0, 1), (0, 2), "added", "others", (0, 3), (0, 4), (1, 1), "spread", (1, 2), "in",
    )


def kernel(
    slots,
    leg_in,
    lon_in,
    obs_w_in,
    span_w_in,
    span_of_in,
    order_in,
    slab_in,
    prod,
    leg,
    lon,
    obs_w,
    span_w,
    span_of,
    order,
    slab,
    table,
    own,
    gath,
    masked,
    parts,
    summed,
    column,
    weighted,
    wcol,
    packed,
    in_sem,
    ring_send,
    ring_recv,
    y_send,
    y_recv,
    c_send,
    c_recv,
):
    chunks = chunks_of(slots)
    compact = slots < SLOTS
    x, yl, core = lax.axis_index("x"), lax.axis_index("yl"), lax.axis_index("core")
    z, yh = lax.axis_index("z"), lax.axis_index("yh")
    row = (x * NYL + yl) * NCORE + core
    mine = z * NYH + yh
    other = 1 - yh
    half = row % 2
    facing_z, facing_y = (row // 4 - z + NZ) % NZ, (row // 2 + yh) % NYH
    away = (facing_z != z) | (facing_y != yh)

    def row_id(k):
        return {"x": k // (NYL * NCORE), "yl": (k // NCORE) % NYL, "core": k % NCORE}

    facing = {"z": facing_z, "yh": facing_y}

    def met(k):
        return ((k // 4 - z + NZ) % NZ) * NYH + (k // 2 + yh) % NYH

    inputs = []
    for i, (source, to) in enumerate(
        (
            (order_in, order),
            (slab_in, slab),
            (lon_in, lon),
            (leg_in, leg),
            (obs_w_in, obs_w),
            (span_w_in, span_w),
            (span_of_in, span_of),
        )
    ):
        copy = pltpu.make_async_copy(source, to, in_sem.at[i])
        copy.start()
        inputs.append(copy)

    barrier = pltpu.get_barrier_semaphore()

    def hello(to):
        pl.semaphore_signal(barrier, inc=1, device_id=to, device_id_type=MESH)

    def hello_row(i, c):
        hello(row_id((row + i) % NROW))
        return c

    hello({"z": (z + 1) % NZ})
    hello({"z": (z + NZ - 1) % NZ})
    hello({"yh": other})

    @pl.when(away)
    def _():
        hello(facing)

    lax.fori_loop(1, NROW, hello_row, 0)

    for copy in inputs[:3]:
        copy.wait()
    base = slab[0]
    tiles = [order[s * NROW + row] for s in range(SLOTS)]
    if compact:
        index = [jnp.int32(0)] * slots
        place, at = [], jnp.int32(0)
        for s in range(SLOTS):
            need = (tiles[s] >= base) & (tiles[s] < TILES)
            hit = jnp.where(need, at, -1)
            for k in range(min(s + 1, slots)):
                index[k] = jnp.where(hit == k, s, index[k])
            place.append(hit)
            at = at + jnp.where(need, 1, 0)
        held = [order[i * NROW + row] for i in index]
    else:
        index, held = list(range(SLOTS)), tiles

    sub = lax.broadcasted_iota(jnp.int32, (8, TILE), 0)
    lane = lax.broadcasted_iota(jnp.int32, (8, TILE), 1)
    for b in range(4):
        own_lon = jnp.zeros((8, TILE), jnp.float32)
        for j in range(8):
            own_lon = jnp.where(sub == j, lon[b * TILE + mine * 8 + j], own_lon)
        for a in range(4):
            k = lane + a * TILE
            m = jnp.where(k > DEGREE, k - (DEGREE + 1), k).astype(jnp.float32)
            table[a, pl.ds(b * 8, 8), :] = jnp.cos(own_lon * m)
    for copy in inputs[3:]:
        copy.wait()

    lane32 = lax.broadcasted_iota(jnp.int32, (SHARD, TILE), 1)

    def design(chunk):
        s0, n = chunks[chunk]
        for s in range(s0, s0 + n):
            t = held[s]
            start = t * TILE - ((t * 111477) >> 18) * (DEGREE + 1)
            a0 = start // TILE
            shift = start - a0 * TILE
            back = (TILE - shift) % TILE
            low = pltpu.roll(table[a0], back, 1)
            high = pltpu.roll(table[a0 + 1], back, 1)
            cosine = jnp.where(lane32 < TILE - shift, low, high)
            values = jnp.concatenate(
                [leg[b, index[s]].astype(jnp.float32) for b in range(4)], axis=0
            )
            value = jnp.where(lane32 < UNK - t * TILE, values * cosine, 0.0)
            own[s] = value.astype(jnp.bfloat16)

    started = []

    def go(copy):
        copy.start()
        started.append(copy)

    def ring(direction, which, hop, chunk, arriving=False):
        s0, n = chunks[chunk]
        sign = 1 if direction == 0 else -1
        src_z = (z - sign * (hop if arriving else hop - 1) + NZ) % NZ
        ref = gath.at[src_z * NYH + (yh if which == 0 else other), pl.ds(s0, n)]
        first = which == 0 and hop == 1 and not arriving
        return pltpu.make_async_remote_copy(
            src_ref=own.at[pl.ds(s0, n)] if first else ref,
            dst_ref=ref,
            send_sem=ring_send.at[direction, which, hop - 1, chunk],
            recv_sem=ring_recv.at[direction, which, hop - 1, chunk],
            device_id={"z": (z + sign + NZ) % NZ},
            device_id_type=MESH,
        )

    def across(far, chunk, arriving=False):
        s0, n = chunks[chunk]
        src_z = (z + 4) % NZ if far else z
        ref = gath.at[src_z * NYH + (other if arriving else yh), pl.ds(s0, n)]
        return pltpu.make_async_remote_copy(
            src_ref=ref if far or arriving else own.at[pl.ds(s0, n)],
            dst_ref=ref,
            send_sem=y_send.at[1 if far else 0, chunk],
            recv_sem=y_recv.at[1 if far else 0, chunk],
            device_id={"yh": other},
            device_id_type=MESH,
        )

    count = range(len(chunks))

    def launch(chunk):
        go(ring(0, 0, 1, chunk))
        go(ring(1, 0, 1, chunk))

    for g in count:
        design(g)

    for q in range(NCOL):
        at, found = jnp.int32(0), jnp.int32(0)
        for s in range(slots):
            hit = held[s] == base + q
            at = jnp.where(hit, s, at)
            found = jnp.where(hit, 1, found)
        got = jnp.where(found == 1, own[at].astype(jnp.float32), 0.0).astype(jnp.bfloat16)
        masked[pl.ds(2 * q, 2)] = got.reshape(2, 16, TILE)

    def ring_round(which, hop):
        for g in count:
            for direction in (0, 1):
                last = hops(which, g)[direction]
                if hop <= last:
                    ring(direction, which, hop, g, True).wait_recv()
                if hop < last:
                    go(ring(direction, which, hop + 1, g))
                if which == 0 and hop == 4 and hop == last:
                    go(across(True, g))

    def row_sends(stage, source, target):
        def send(i, c):
            k = (row + i) % NROW
            pltpu.make_async_remote_copy(
                src_ref=source(k),
                dst_ref=target,
                send_sem=c_send.at[stage],
                recv_sem=c_recv.at[stage],
                device_id=row_id(k),
                device_id_type=MESH,
            ).start()
            return c

        lax.fori_loop(1, NROW, send, 0)

    def row_wait(stage, buffer):
        lines = buffer.at[pl.ds(0, NROW - 1)]
        pltpu.make_async_copy(lines, lines, c_recv.at[stage]).wait()
        pltpu.make_async_copy(lines, lines, c_send.at[stage]).wait()

    def columns_out():
        row_sends(0, lambda k: masked.at[2 * met(k) + k % 2], parts.at[row])
        parts[row] = masked[2 * met(row) + half]

    cross = pltpu.make_async_remote_copy(
        src_ref=summed,
        dst_ref=column.at[row],
        send_sem=c_send.at[1],
        recv_sem=c_recv.at[1],
        device_id=facing,
        device_id_type=MESH,
    )

    def columns_added():
        row_wait(0, parts)
        total = parts[0].astype(jnp.float32)
        for k in range(1, NROW):
            total = total + parts[k].astype(jnp.float32)
        summed[...] = total.astype(jnp.bfloat16)

        @pl.when(away)
        def _():
            cross.start()

        @pl.when(jnp.logical_not(away))
        def _():
            column[row] = summed[...]

    def columns_spread():
        @pl.when(away)
        def _():
            cross.wait_send()
            pltpu.make_async_copy(column.at[row], column.at[row], c_recv.at[1]).wait()

        row_sends(2, lambda k: column.at[row], column.at[row])

    def columns_in():
        row_wait(2, column)
        for c in range(NCOL):
            k = ((c // NYH + z) % NZ) * 4 + ((c % NYH + yh) % NYH) * 2
            col = column[pl.ds(k, 2)].reshape(SHARD, TILE).astype(jnp.float32)
            value = col * wcol[c].reshape(SHARD, TILE)
            weighted[pl.ds(c * SHARD, SHARD)] = value.astype(jnp.bfloat16)

    def others_out():
        for g in count:
            across(False, g, True).wait_recv()
            go(ring(0, 1, 1, g))
            go(ring(1, 1, 1, g))

    pl.semaphore_wait(barrier, 3 + (NROW - 1) + jnp.where(away, 1, 0))
    for g in count:
        launch(g)
    columns_out()
    for g in count:
        go(across(False, g))

    weights = jnp.zeros((4, TILE), jnp.float32)
    for g in range(8):
        weights = jnp.where(span_of[...] == g, span_w[g], weights)
    weights = obs_w[...] * weights * (0.25 / math.sqrt(OBS))
    for b in range(4):
        wide = jnp.broadcast_to(weights[b : b + 1, :], (TILE, TILE))
        wcol[:, b] = jnp.transpose(wide).reshape(NCOL, 8, TILE)
    gath[mine] = own[...]

    steps = {
        "added": columns_added,
        "spread": columns_spread,
        "in": columns_in,
        "others": others_out,
    }
    for step in plan_of(slots):
        if step in steps:
            steps[step]()
        else:
            ring_round(*step)

    target = base + mine
    goal = packed if compact else prod
    weight_block = weighted[...]
    for g in count:
        ring(0, 1, 3, g, True).wait_recv()
        ring(1, 1, 3, g, True).wait_recv()
        across(True, g, True).wait_recv()
        s0, n = chunks[g]
        for k in range(s0, s0 + n):
            product = lax.dot_general(
                gath[:, k].reshape(OBS, TILE),
                weight_block,
                (((0,), (0,)), ((), ())),
                preferred_element_type=jnp.float32,
            )
            goal[k] = product if compact else jnp.where(tiles[k] >= target, product, 0.0)
    if compact:
        for s in range(SLOTS):
            keep = (place[s] >= 0) & (tiles[s] >= target)
            prod[s] = jnp.where(keep, packed[jnp.clip(place[s], 0, slots - 1)], 0.0)
    for copy in started:
        copy.wait_send()


def product_of(slots, identity):
    hbm = pl.BlockSpec(memory_space=pltpu.HBM)
    bf16, f32, i32 = jnp.bfloat16, jnp.float32, jnp.int32
    dma = pltpu.SemaphoreType.DMA
    pieces = len(chunks_of(slots))
    return pl.pallas_call(
        functools.partial(kernel, slots),
        out_shape=jax.ShapeDtypeStruct((SLOTS, TILE, TILE), f32),
        in_specs=[hbm] * 7,
        out_specs=pl.BlockSpec(memory_space=pltpu.VMEM),
        scratch_shapes=[
            pltpu.VMEM((4, SLOTS, 8, TILE), bf16),
            pltpu.SMEM((OBS,), f32),
            pltpu.VMEM((4, TILE), f32),
            pltpu.SMEM((8,), f32),
            pltpu.VMEM((4, TILE), i32),
            pltpu.SMEM((SLOTS * NROW,), i32),
            pltpu.SMEM((1,), i32),
            pltpu.VMEM((4, SHARD, TILE), f32),
            pltpu.VMEM((slots, SHARD, TILE), bf16),
            pltpu.VMEM((NCOL, slots, SHARD, TILE), bf16),
            pltpu.VMEM((NROW, 16, TILE), bf16),
            pltpu.VMEM((NROW, 16, TILE), bf16),
            pltpu.VMEM((16, TILE), bf16),
            pltpu.VMEM((NROW, 16, TILE), bf16),
            pltpu.VMEM((OBS, TILE), bf16),
            pltpu.VMEM((NCOL, 4, 8, TILE), f32),
            pltpu.VMEM((slots, TILE, TILE), f32),
            dma((7,)),
            dma((2, 2, 4, pieces)),
            dma((2, 2, 4, pieces)),
            dma((2, pieces)),
            dma((2, pieces)),
            dma((3,)),
            dma((3,)),
        ],
        compiler_params=pltpu.CompilerParams(
            collective_id=identity, has_side_effects=True, vmem_limit_bytes=24 * 1024 * 1024
        ),
    )


def per_device(
    legendre, longitude, obs_weight, span_weight, span_of, tile_order, slab_start, resident
):
    leg = legendre.reshape(4, 8, SLOTS, TILE).transpose(0, 2, 1, 3)
    given = (
        leg,
        longitude,
        obs_weight.reshape(4, TILE),
        span_weight,
        span_of.reshape(4, TILE),
        tile_order,
        slab_start,
    )
    if len(SIZES) > 1:
        reached = (tile_order >= slab_start) & (tile_order < TILES)
        counts = jnp.sum(reached.reshape(SLOTS, NROW).astype(jnp.int32), axis=0)
        level = jnp.max(sum((counts > size).astype(jnp.int32) for size in SIZES[:-1]))
        product = lax.switch(level, [product_of(size, i) for i, size in enumerate(SIZES)], *given)
    else:
        product = product_of(SIZES[0], 0)(*given)
    return resident + product.reshape(resident.shape)


def solution(mesh):
    torus = Mesh(
        mesh.devices.reshape(NX, NYL, NCORE, NZ, NYH), ("x", "yl", "core", "z", "yh")
    )
    rows, cols = ("x", "yl", "core"), ("z", "yh")
    return jax.shard_map(
        per_device,
        mesh=torus,
        in_specs=(
            P(None, cols, None, rows, None),
            P(),
            P(),
            P(),
            P(),
            P(),
            P(),
            P(None, rows, cols, None, None),
        ),
        out_specs=P(None, rows, cols, None, None),
        check_vma=False,
    )
```

```python
import functools
import math

import jax
import jax.numpy as jnp
from jax import lax
from jax.experimental import pallas as pl
from jax.experimental.pallas import tpu as pltpu
from jax.sharding import Mesh
from jax.sharding import PartitionSpec as P

DEGREE = 300
UNK = 90600
TILES = 708
MESH = pl.DeviceIdType.MESH
NX, NYL, NCORE, NZ, NYH = 4, 4, 2, 8, 2
NROW = NX * NYL * NCORE
NCOL = NZ * NYH
SLOTS = 23
TILE = 128
OBS = 512
SHARD = OBS // NCOL
SIZES = (10, 14, 17, 20, 23)


def chunks_of(slots):
    count = min(4, slots)
    edges = [slots * i // count for i in range(count + 1)]
    return tuple((a, b - a) for a, b in zip(edges[:-1], edges[1:]))


def hops(which, chunk):
    if which == 1:
        return (3, 3)
    return (4, 3) if chunk % 2 == 0 else (3, 4)


PLAN = (
    (0, 1), "halfway", (0, 2), "added", (0, 3), "others", (0, 4), "spread", "far",
    (1, 1), "across", (1, 2), "in",
)


def kernel(
    slots,
    leg_in,
    lon_in,
    obs_w_in,
    span_w_in,
    span_of_in,
    order_in,
    slab_in,
    prod,
    leg,
    lon,
    obs_w,
    span_w,
    span_of,
    order,
    slab,
    table,
    own,
    gath,
    masked,
    parts,
    middle,
    line,
    summed,
    column,
    weighted,
    wcol,
    packed,
    in_sem,
    ring_send,
    ring_recv,
    y_send,
    y_recv,
    c_send,
    c_recv,
):
    chunks = chunks_of(slots)
    compact = slots < SLOTS
    x, yl, core = lax.axis_index("x"), lax.axis_index("yl"), lax.axis_index("core")
    z, yh = lax.axis_index("z"), lax.axis_index("yh")
    row = (x * NYL + yl) * NCORE + core
    mine = z * NYH + yh
    other = 1 - yh
    rank = (x * NCORE + core) * NYL + yl
    lined = [({"yl": (yl + i) % NYL}, (yl + i) % NYL) for i in (2, 1, 3)]
    crossed = []
    for dx in (2, 1, 3, 0):
        for dc in (1, 0):
            if dx or dc:
                to = {"x": (x + dx) % NX, "core": (core + dc) % NCORE}
                crossed.append((to, to["x"] * NCORE + to["core"]))

    facing_z, facing_y = (rank // 4 - z + NZ) % NZ, (rank // 2 + yh) % NYH
    away = (facing_z != z) | (facing_y != yh)
    facing = {"z": facing_z, "yh": facing_y}

    inputs = []
    for i, (source, to) in enumerate(
        (
            (order_in, order),
            (slab_in, slab),
            (lon_in, lon),
            (leg_in, leg),
            (obs_w_in, obs_w),
            (span_w_in, span_w),
            (span_of_in, span_of),
        )
    ):
        copy = pltpu.make_async_copy(source, to, in_sem.at[i])
        copy.start()
        inputs.append(copy)

    barrier = pltpu.get_barrier_semaphore()

    def hello(to):
        pl.semaphore_signal(barrier, inc=1, device_id=to, device_id_type=MESH)

    for to, _ in lined + crossed:
        hello(to)
    hello({"z": (z + 1) % NZ})
    hello({"z": (z + NZ - 1) % NZ})
    hello({"yh": other})

    @pl.when(away)
    def _():
        hello(facing)

    for copy in inputs[:3]:
        copy.wait()
    base = slab[0]
    tiles = [order[s * NROW + row] for s in range(SLOTS)]
    if compact:
        index = [jnp.int32(0)] * slots
        place, at = [], jnp.int32(0)
        for s in range(SLOTS):
            need = (tiles[s] >= base) & (tiles[s] < TILES)
            hit = jnp.where(need, at, -1)
            for k in range(min(s + 1, slots)):
                index[k] = jnp.where(hit == k, s, index[k])
            place.append(hit)
            at = at + jnp.where(need, 1, 0)
        held = [order[i * NROW + row] for i in index]
    else:
        index, held = list(range(SLOTS)), tiles

    sub = lax.broadcasted_iota(jnp.int32, (8, TILE), 0)
    lane = lax.broadcasted_iota(jnp.int32, (8, TILE), 1)
    for b in range(4):
        own_lon = jnp.zeros((8, TILE), jnp.float32)
        for j in range(8):
            own_lon = jnp.where(sub == j, lon[b * TILE + mine * 8 + j], own_lon)
        for a in range(4):
            k = lane + a * TILE
            m = jnp.where(k > DEGREE, k - (DEGREE + 1), k).astype(jnp.float32)
            table[a, pl.ds(b * 8, 8), :] = jnp.cos(own_lon * m)
    for copy in inputs[3:]:
        copy.wait()

    lane32 = lax.broadcasted_iota(jnp.int32, (SHARD, TILE), 1)

    def design(chunk):
        s0, n = chunks[chunk]
        for s in range(s0, s0 + n):
            t = held[s]
            start = t * TILE - ((t * 111477) >> 18) * (DEGREE + 1)
            a0 = start // TILE
            shift = start - a0 * TILE
            back = (TILE - shift) % TILE
            low = pltpu.roll(table[a0], back, 1)
            high = pltpu.roll(table[a0 + 1], back, 1)
            cosine = jnp.where(lane32 < TILE - shift, low, high)
            values = jnp.concatenate(
                [leg[b, index[s]].astype(jnp.float32) for b in range(4)], axis=0
            )
            value = jnp.where(lane32 < UNK - t * TILE, values * cosine, 0.0)
            own[s] = value.astype(jnp.bfloat16)

    started = []

    def go(copy):
        copy.start()
        started.append(copy)

    def ring(direction, which, hop, chunk, arriving=False):
        s0, n = chunks[chunk]
        sign = 1 if direction == 0 else -1
        src_z = (z - sign * (hop if arriving else hop - 1) + NZ) % NZ
        ref = gath.at[src_z * NYH + (yh if which == 0 else other), pl.ds(s0, n)]
        first = which == 0 and hop == 1 and not arriving
        return pltpu.make_async_remote_copy(
            src_ref=own.at[pl.ds(s0, n)] if first else ref,
            dst_ref=ref,
            send_sem=ring_send.at[direction, which, hop - 1, chunk],
            recv_sem=ring_recv.at[direction, which, hop - 1, chunk],
            device_id={"z": (z + sign + NZ) % NZ},
            device_id_type=MESH,
        )

    def across(far, chunk, arriving=False):
        s0, n = chunks[chunk]
        src_z = (z + 4) % NZ if far else z
        ref = gath.at[src_z * NYH + (other if arriving else yh), pl.ds(s0, n)]
        return pltpu.make_async_remote_copy(
            src_ref=ref if far or arriving else own.at[pl.ds(s0, n)],
            dst_ref=ref,
            send_sem=y_send.at[1 if far else 0, chunk],
            recv_sem=y_recv.at[1 if far else 0, chunk],
            device_id={"yh": other},
            device_id_type=MESH,
        )

    count = range(len(chunks))

    def launch(chunk):
        go(ring(0, 0, 1, chunk))
        go(ring(1, 0, 1, chunk))

    for g in count:
        design(g)

    for q in range(NCOL):
        at, found = jnp.int32(0), jnp.int32(0)
        for s in range(slots):
            hit = held[s] == base + q
            at = jnp.where(hit, s, at)
            found = jnp.where(hit, 1, found)
        got = jnp.where(found == 1, own[at].astype(jnp.float32), 0.0).astype(jnp.bfloat16)
        k = ((q // NYH + z) % NZ) * 4 + ((q % NYH + yh) % NYH) * 2
        masked[pl.ds(k, 2)] = got.reshape(2, 16, TILE)

    def ring_round(which, hop):
        for g in count:
            for direction in (0, 1):
                last = hops(which, g)[direction]
                if hop <= last:
                    ring(direction, which, hop, g, True).wait_recv()
                if hop < last:
                    go(ring(direction, which, hop + 1, g))

    def sends(stage, peers, source, target):
        for to, k in peers:
            pltpu.make_async_remote_copy(
                src_ref=source(k),
                dst_ref=target,
                send_sem=c_send.at[stage],
                recv_sem=c_recv.at[stage],
                device_id=to,
                device_id_type=MESH,
            ).start()

    def arrived(stage, buffer, pieces):
        lines = buffer.at[pl.ds(0, pieces)]
        pltpu.make_async_copy(lines, lines, c_recv.at[stage]).wait()
        pltpu.make_async_copy(lines, lines, c_send.at[stage]).wait()

    def sum_of(values):
        total = values[0].astype(jnp.float32)
        for value in values[1:]:
            total = total + value.astype(jnp.float32)
        return total.astype(jnp.bfloat16)

    block = pl.ds((x * NCORE + core) * NYL, NYL)

    def columns_out():
        sends(0, crossed, lambda k: masked.at[pl.ds(k * NYL, NYL)], parts.at[block])
        parts[block] = masked[block]

    cross = pltpu.make_async_remote_copy(
        src_ref=summed,
        dst_ref=column.at[rank],
        send_sem=c_send.at[2],
        recv_sem=c_recv.at[2],
        device_id=facing,
        device_id_type=MESH,
    )

    def columns_halfway():
        arrived(0, parts, 7 * NYL)
        for j in range(NYL):
            middle[j] = sum_of([parts[k * NYL + j] for k in range(NX * NCORE)])
        sends(1, lined, lambda k: middle.at[k], line.at[yl])
        line[yl] = middle[yl]

    def columns_added():
        arrived(1, line, NYL - 1)
        summed[...] = sum_of([line[j] for j in range(NYL)])

        @pl.when(away)
        def _():
            cross.start()

        @pl.when(jnp.logical_not(away))
        def _():
            column[rank] = summed[...]

    def columns_spread():
        @pl.when(away)
        def _():
            cross.wait_send()
            pltpu.make_async_copy(column.at[rank], column.at[rank], c_recv.at[2]).wait()

        sends(3, lined, lambda k: column.at[rank], column.at[rank])

    def columns_across():
        arrived(3, line, NYL - 1)
        sends(4, crossed, lambda k: column.at[block], column.at[block])

    def columns_in():
        arrived(4, parts, 7 * NYL)
        for c in range(NCOL):
            k = ((c // NYH + z) % NZ) * 4 + ((c % NYH + yh) % NYH) * 2
            col = column[pl.ds(k, 2)].reshape(SHARD, TILE).astype(jnp.float32)
            value = col * wcol[c].reshape(SHARD, TILE)
            weighted[pl.ds(c * SHARD, SHARD)] = value.astype(jnp.bfloat16)

    def others_out():
        for g in count:
            across(False, g, True).wait_recv()
            go(ring(0, 1, 1, g))
            go(ring(1, 1, 1, g))

    def far_out():
        for g in count:
            go(across(True, g))

    pl.semaphore_wait(barrier, 3 + len(lined + crossed) + jnp.where(away, 1, 0))
    for g in count:
        launch(g)
    columns_out()
    for g in count:
        go(across(False, g))

    weights = jnp.zeros((4, TILE), jnp.float32)
    for g in range(8):
        weights = jnp.where(span_of[...] == g, span_w[g], weights)
    weights = obs_w[...] * weights * (0.25 / math.sqrt(OBS))
    for b in range(4):
        wide = jnp.broadcast_to(weights[b : b + 1, :], (TILE, TILE))
        wcol[:, b] = jnp.transpose(wide).reshape(NCOL, 8, TILE)
    gath[mine] = own[...]

    steps = {
        "halfway": columns_halfway,
        "added": columns_added,
        "across": columns_across,
        "spread": columns_spread,
        "in": columns_in,
        "others": others_out,
        "far": far_out,
    }
    for step in PLAN:
        if step in steps:
            steps[step]()
        else:
            ring_round(*step)

    target = base + mine
    goal = packed if compact else prod
    weight_block = weighted[...]
    for g in count:
        ring(0, 1, 3, g, True).wait_recv()
        ring(1, 1, 3, g, True).wait_recv()
        across(True, g, True).wait_recv()
        s0, n = chunks[g]
        for k in range(s0, s0 + n):
            product = lax.dot_general(
                gath[:, k].reshape(OBS, TILE),
                weight_block,
                (((0,), (0,)), ((), ())),
                preferred_element_type=jnp.float32,
            )
            goal[k] = product if compact else jnp.where(tiles[k] >= target, product, 0.0)
    if compact:
        for s in range(SLOTS):
            keep = (place[s] >= 0) & (tiles[s] >= target)
            prod[s] = jnp.where(keep, packed[jnp.clip(place[s], 0, slots - 1)], 0.0)
    for copy in started:
        copy.wait_send()


def product_of(slots, identity):
    hbm = pl.BlockSpec(memory_space=pltpu.HBM)
    bf16, f32, i32 = jnp.bfloat16, jnp.float32, jnp.int32
    dma = pltpu.SemaphoreType.DMA
    pieces = len(chunks_of(slots))
    return pl.pallas_call(
        functools.partial(kernel, slots),
        out_shape=jax.ShapeDtypeStruct((SLOTS, TILE, TILE), f32),
        in_specs=[hbm] * 7,
        out_specs=pl.BlockSpec(memory_space=pltpu.VMEM),
        scratch_shapes=[
            pltpu.VMEM((4, SLOTS, 8, TILE), bf16),
            pltpu.SMEM((OBS,), f32),
            pltpu.VMEM((4, TILE), f32),
            pltpu.SMEM((8,), f32),
            pltpu.VMEM((4, TILE), i32),
            pltpu.SMEM((SLOTS * NROW,), i32),
            pltpu.SMEM((1,), i32),
            pltpu.VMEM((4, SHARD, TILE), f32),
            pltpu.VMEM((slots, SHARD, TILE), bf16),
            pltpu.VMEM((NCOL, slots, SHARD, TILE), bf16),
            pltpu.VMEM((NROW, 16, TILE), bf16),
            pltpu.VMEM((NROW, 16, TILE), bf16),
            pltpu.VMEM((NYL, 16, TILE), bf16),
            pltpu.VMEM((NYL, 16, TILE), bf16),
            pltpu.VMEM((16, TILE), bf16),
            pltpu.VMEM((NROW, 16, TILE), bf16),
            pltpu.VMEM((OBS, TILE), bf16),
            pltpu.VMEM((NCOL, 4, 8, TILE), f32),
            pltpu.VMEM((slots, TILE, TILE), f32),
            dma((7,)),
            dma((2, 2, 4, pieces)),
            dma((2, 2, 4, pieces)),
            dma((2, pieces)),
            dma((2, pieces)),
            dma((5,)),
            dma((5,)),
        ],
        compiler_params=pltpu.CompilerParams(
            collective_id=identity, has_side_effects=True, vmem_limit_bytes=24 * 1024 * 1024
        ),
    )


def per_device(
    legendre, longitude, obs_weight, span_weight, span_of, tile_order, slab_start, resident
):
    leg = legendre.reshape(4, 8, SLOTS, TILE).transpose(0, 2, 1, 3)
    given = (
        leg,
        longitude,
        obs_weight.reshape(4, TILE),
        span_weight,
        span_of.reshape(4, TILE),
        tile_order,
        slab_start,
    )
    if len(SIZES) > 1:
        reached = (tile_order >= slab_start) & (tile_order < TILES)
        counts = jnp.sum(reached.reshape(SLOTS, NROW).astype(jnp.int32), axis=0)
        level = jnp.max(sum((counts > size).astype(jnp.int32) for size in SIZES[:-1]))
        product = lax.switch(level, [product_of(size, i) for i, size in enumerate(SIZES)], *given)
    else:
        product = product_of(SIZES[0], 0)(*given)
    return resident + product.reshape(resident.shape)


def solution(mesh):
    torus = Mesh(
        mesh.devices.reshape(NX, NYL, NCORE, NZ, NYH), ("x", "yl", "core", "z", "yh")
    )
    rows, cols = ("x", "yl", "core"), ("z", "yh")
    return jax.shard_map(
        per_device,
        mesh=torus,
        in_specs=(
            P(None, cols, None, rows, None),
            P(),
            P(),
            P(),
            P(),
            P(),
            P(),
            P(None, rows, cols, None, None),
        ),
        out_specs=P(None, rows, cols, None, None),
        check_vma=False,
    )
```

```python
import functools
import math

import jax
import jax.numpy as jnp
from jax import lax
from jax.experimental import pallas as pl
from jax.experimental.pallas import tpu as pltpu
from jax.sharding import Mesh
from jax.sharding import PartitionSpec as P

DEGREE = 300
UNK = 90600
TILES = 708
MESH = pl.DeviceIdType.MESH
NX, NYL, NCORE, NZ, NYH = 4, 4, 2, 8, 2
NROW = NX * NYL * NCORE
NCOL = NZ * NYH
SLOTS = 23
TILE = 128
OBS = 512
SHARD = OBS // NCOL
SIZES = (10, 14, 17, 20, 23)


def chunks_of(slots):
    count = min(4, slots)
    edges = [slots * i // count for i in range(count + 1)]
    return tuple((a, b - a) for a, b in zip(edges[:-1], edges[1:]))


def hops(which, chunk):
    if which == 1:
        return (3, 3)
    return (4, 3) if chunk % 2 == 0 else (3, 4)


PLAN = (
    (0, 1), "halfway", (0, 2), "added", (0, 3), "others", (0, 4), "spread", "far",
    (1, 1), "across", (1, 2), "in",
)


def kernel(
    slots,
    leg_in,
    lon_in,
    obs_w_in,
    span_w_in,
    span_of_in,
    order_in,
    slab_in,
    prod,
    leg,
    lon,
    obs_w,
    span_w,
    span_of,
    order,
    slab,
    table,
    own,
    gath,
    masked,
    parts,
    middle,
    line,
    summed,
    column,
    weighted,
    wcol,
    packed,
    in_sem,
    ring_send,
    ring_recv,
    y_send,
    y_recv,
    c_send,
    c_recv,
):
    chunks = chunks_of(slots)
    compact = slots < SLOTS
    x, yl, core = lax.axis_index("x"), lax.axis_index("yl"), lax.axis_index("core")
    z, yh = lax.axis_index("z"), lax.axis_index("yh")
    row = (x * NYL + yl) * NCORE + core
    mine = z * NYH + yh
    other = 1 - yh
    rank = (x * NCORE + core) * NYL + yl
    lined = [({"yl": (yl + i) % NYL}, (yl + i) % NYL) for i in (2, 1, 3)]
    crossed = []
    for dx in (2, 1, 3, 0):
        for dc in (1, 0):
            if dx or dc:
                to = {"x": (x + dx) % NX, "core": (core + dc) % NCORE}
                crossed.append((to, to["x"] * NCORE + to["core"]))

    facing_z, facing_y = (rank // 4 - z + NZ) % NZ, (rank // 2 + yh) % NYH
    away = (facing_z != z) | (facing_y != yh)
    facing = {"z": facing_z, "yh": facing_y}

    barrier = pltpu.get_barrier_semaphore()

    def hello(to):
        pl.semaphore_signal(barrier, inc=1, device_id=to, device_id_type=MESH)

    hello({"z": (z + 1) % NZ})
    hello({"z": (z + NZ - 1) % NZ})
    hello({"yh": other})
    for to, _ in lined + crossed:
        hello(to)

    @pl.when(away)
    def _():
        hello(facing)

    inputs = []
    for i, (source, to) in enumerate(
        (
            (order_in, order),
            (slab_in, slab),
            (lon_in, lon),
            (leg_in, leg),
            (obs_w_in, obs_w),
            (span_w_in, span_w),
            (span_of_in, span_of),
        )
    ):
        copy = pltpu.make_async_copy(source, to, in_sem.at[i])
        copy.start()
        inputs.append(copy)

    for copy in inputs[:3]:
        copy.wait()
    base = slab[0]
    tiles = [order[s * NROW + row] for s in range(SLOTS)]
    if compact:
        index = [jnp.int32(0)] * slots
        place, at = [], jnp.int32(0)
        for s in range(SLOTS):
            need = (tiles[s] >= base) & (tiles[s] < TILES)
            hit = jnp.where(need, at, -1)
            for k in range(min(s + 1, slots)):
                index[k] = jnp.where(hit == k, s, index[k])
            place.append(hit)
            at = at + jnp.where(need, 1, 0)
        held = [order[i * NROW + row] for i in index]
    else:
        index, held = list(range(SLOTS)), tiles

    sub = lax.broadcasted_iota(jnp.int32, (8, TILE), 0)
    lane = lax.broadcasted_iota(jnp.int32, (8, TILE), 1)
    for b in range(4):
        own_lon = jnp.zeros((8, TILE), jnp.float32)
        for j in range(8):
            own_lon = jnp.where(sub == j, lon[b * TILE + mine * 8 + j], own_lon)
        for a in range(4):
            k = lane + a * TILE
            m = jnp.where(k > DEGREE, k - (DEGREE + 1), k).astype(jnp.float32)
            table[a, pl.ds(b * 8, 8), :] = jnp.cos(own_lon * m)
    for copy in inputs[3:]:
        copy.wait()

    lane32 = lax.broadcasted_iota(jnp.int32, (SHARD, TILE), 1)

    def design(chunk):
        s0, n = chunks[chunk]
        for s in range(s0, s0 + n):
            t = held[s]
            start = t * TILE - ((t * 111477) >> 18) * (DEGREE + 1)
            a0 = start // TILE
            shift = start - a0 * TILE
            back = (TILE - shift) % TILE
            low = pltpu.roll(table[a0], back, 1)
            high = pltpu.roll(table[a0 + 1], back, 1)
            cosine = jnp.where(lane32 < TILE - shift, low, high)
            values = jnp.concatenate(
                [leg[b, index[s]].astype(jnp.float32) for b in range(4)], axis=0
            )
            value = jnp.where(lane32 < UNK - t * TILE, values * cosine, 0.0)
            own[s] = value.astype(jnp.bfloat16)

    started = []

    def go(copy):
        copy.start()
        started.append(copy)

    def ring(direction, which, hop, chunk, arriving=False):
        s0, n = chunks[chunk]
        sign = 1 if direction == 0 else -1
        src_z = (z - sign * (hop if arriving else hop - 1) + NZ) % NZ
        ref = gath.at[src_z * NYH + (yh if which == 0 else other), pl.ds(s0, n)]
        first = which == 0 and hop == 1 and not arriving
        return pltpu.make_async_remote_copy(
            src_ref=own.at[pl.ds(s0, n)] if first else ref,
            dst_ref=ref,
            send_sem=ring_send.at[direction, which, hop - 1, chunk],
            recv_sem=ring_recv.at[direction, which, hop - 1, chunk],
            device_id={"z": (z + sign + NZ) % NZ},
            device_id_type=MESH,
        )

    def across(far, chunk, arriving=False):
        s0, n = chunks[chunk]
        src_z = (z + 4) % NZ if far else z
        ref = gath.at[src_z * NYH + (other if arriving else yh), pl.ds(s0, n)]
        return pltpu.make_async_remote_copy(
            src_ref=ref if far or arriving else own.at[pl.ds(s0, n)],
            dst_ref=ref,
            send_sem=y_send.at[1 if far else 0, chunk],
            recv_sem=y_recv.at[1 if far else 0, chunk],
            device_id={"yh": other},
            device_id_type=MESH,
        )

    count = range(len(chunks))

    def launch(chunk):
        go(ring(0, 0, 1, chunk))
        go(ring(1, 0, 1, chunk))

    for g in count:
        design(g)

    for q in range(NCOL):
        at, found = jnp.int32(0), jnp.int32(0)
        for s in range(slots):
            hit = held[s] == base + q
            at = jnp.where(hit, s, at)
            found = jnp.where(hit, 1, found)
        got = jnp.where(found == 1, own[at].astype(jnp.float32), 0.0).astype(jnp.bfloat16)
        k = ((q // NYH + z) % NZ) * 4 + ((q % NYH + yh) % NYH) * 2
        masked[pl.ds(k, 2)] = got.reshape(2, 16, TILE)

    def ring_round(which, hop):
        for g in count:
            for direction in (0, 1):
                last = hops(which, g)[direction]
                if hop <= last:
                    ring(direction, which, hop, g, True).wait_recv()
                if hop < last:
                    go(ring(direction, which, hop + 1, g))

    def sends(stage, peers, source, target):
        for to, k in peers:
            pltpu.make_async_remote_copy(
                src_ref=source(k),
                dst_ref=target,
                send_sem=c_send.at[stage],
                recv_sem=c_recv.at[stage],
                device_id=to,
                device_id_type=MESH,
            ).start()

    def arrived(stage, buffer, pieces):
        lines = buffer.at[pl.ds(0, pieces)]
        pltpu.make_async_copy(lines, lines, c_recv.at[stage]).wait()
        pltpu.make_async_copy(lines, lines, c_send.at[stage]).wait()

    def sum_of(values):
        total = values[0].astype(jnp.float32)
        for value in values[1:]:
            total = total + value.astype(jnp.float32)
        return total.astype(jnp.bfloat16)

    block = pl.ds((x * NCORE + core) * NYL, NYL)

    def columns_out():
        sends(0, crossed, lambda k: masked.at[pl.ds(k * NYL, NYL)], parts.at[block])
        parts[block] = masked[block]

    cross = pltpu.make_async_remote_copy(
        src_ref=summed,
        dst_ref=column.at[rank],
        send_sem=c_send.at[2],
        recv_sem=c_recv.at[2],
        device_id=facing,
        device_id_type=MESH,
    )

    def columns_halfway():
        arrived(0, parts, 7 * NYL)
        for j in range(NYL):
            middle[j] = sum_of([parts[k * NYL + j] for k in range(NX * NCORE)])
        sends(1, lined, lambda k: middle.at[k], line.at[yl])
        line[yl] = middle[yl]

    def columns_added():
        arrived(1, line, NYL - 1)
        summed[...] = sum_of([line[j] for j in range(NYL)])

        @pl.when(away)
        def _():
            cross.start()

        @pl.when(jnp.logical_not(away))
        def _():
            column[rank] = summed[...]

    def columns_spread():
        @pl.when(away)
        def _():
            cross.wait_send()
            pltpu.make_async_copy(column.at[rank], column.at[rank], c_recv.at[2]).wait()

        sends(3, lined, lambda k: column.at[rank], column.at[rank])

    def columns_across():
        arrived(3, line, NYL - 1)
        sends(4, crossed, lambda k: column.at[block], column.at[block])

    def columns_in():
        arrived(4, parts, 7 * NYL)
        for c in range(NCOL):
            k = ((c // NYH + z) % NZ) * 4 + ((c % NYH + yh) % NYH) * 2
            col = column[pl.ds(k, 2)].reshape(SHARD, TILE).astype(jnp.float32)
            value = col * wcol[c].reshape(SHARD, TILE)
            weighted[pl.ds(c * SHARD, SHARD)] = value.astype(jnp.bfloat16)

    def others_out():
        for g in count:
            across(False, g, True).wait_recv()
            go(ring(0, 1, 1, g))
            go(ring(1, 1, 1, g))

    def far_out():
        for g in count:
            go(across(True, g))

    pl.semaphore_wait(barrier, 3 + len(lined + crossed) + jnp.where(away, 1, 0))
    for g in count:
        launch(g)
    columns_out()
    for g in count:
        go(across(False, g))

    weights = jnp.zeros((4, TILE), jnp.float32)
    for g in range(8):
        weights = jnp.where(span_of[...] == g, span_w[g], weights)
    weights = obs_w[...] * weights * (0.25 / math.sqrt(OBS))
    for b in range(4):
        wide = jnp.broadcast_to(weights[b : b + 1, :], (TILE, TILE))
        wcol[:, b] = jnp.transpose(wide).reshape(NCOL, 8, TILE)
    gath[mine] = own[...]

    steps = {
        "halfway": columns_halfway,
        "added": columns_added,
        "across": columns_across,
        "spread": columns_spread,
        "in": columns_in,
        "others": others_out,
        "far": far_out,
    }
    for step in PLAN:
        if step in steps:
            steps[step]()
        else:
            ring_round(*step)

    target = base + mine
    goal = packed if compact else prod
    weight_block = weighted[...]
    for g in count:
        ring(0, 1, 3, g, True).wait_recv()
        ring(1, 1, 3, g, True).wait_recv()
        across(True, g, True).wait_recv()
        s0, n = chunks[g]
        for k in range(s0, s0 + n):
            product = lax.dot_general(
                gath[:, k].reshape(OBS, TILE),
                weight_block,
                (((0,), (0,)), ((), ())),
                preferred_element_type=jnp.float32,
            )
            goal[k] = product if compact else jnp.where(tiles[k] >= target, product, 0.0)
    if compact:
        for s in range(SLOTS):
            keep = (place[s] >= 0) & (tiles[s] >= target)
            prod[s] = jnp.where(keep, packed[jnp.clip(place[s], 0, slots - 1)], 0.0)
    for copy in started:
        copy.wait_send()


def product_of(slots, identity):
    hbm = pl.BlockSpec(memory_space=pltpu.HBM)
    bf16, f32, i32 = jnp.bfloat16, jnp.float32, jnp.int32
    dma = pltpu.SemaphoreType.DMA
    pieces = len(chunks_of(slots))
    return pl.pallas_call(
        functools.partial(kernel, slots),
        out_shape=jax.ShapeDtypeStruct((SLOTS, TILE, TILE), f32),
        in_specs=[hbm] * 7,
        out_specs=pl.BlockSpec(memory_space=pltpu.VMEM),
        scratch_shapes=[
            pltpu.VMEM((4, SLOTS, 8, TILE), bf16),
            pltpu.SMEM((OBS,), f32),
            pltpu.VMEM((4, TILE), f32),
            pltpu.SMEM((8,), f32),
            pltpu.VMEM((4, TILE), i32),
            pltpu.SMEM((SLOTS * NROW,), i32),
            pltpu.SMEM((1,), i32),
            pltpu.VMEM((4, SHARD, TILE), f32),
            pltpu.VMEM((slots, SHARD, TILE), bf16),
            pltpu.VMEM((NCOL, slots, SHARD, TILE), bf16),
            pltpu.VMEM((NROW, 16, TILE), bf16),
            pltpu.VMEM((NROW, 16, TILE), bf16),
            pltpu.VMEM((NYL, 16, TILE), bf16),
            pltpu.VMEM((NYL, 16, TILE), bf16),
            pltpu.VMEM((16, TILE), bf16),
            pltpu.VMEM((NROW, 16, TILE), bf16),
            pltpu.VMEM((OBS, TILE), bf16),
            pltpu.VMEM((NCOL, 4, 8, TILE), f32),
            pltpu.VMEM((slots, TILE, TILE), f32),
            dma((7,)),
            dma((2, 2, 4, pieces)),
            dma((2, 2, 4, pieces)),
            dma((2, pieces)),
            dma((2, pieces)),
            dma((5,)),
            dma((5,)),
        ],
        compiler_params=pltpu.CompilerParams(
            collective_id=identity, has_side_effects=True, vmem_limit_bytes=24 * 1024 * 1024
        ),
    )


def per_device(
    legendre, longitude, obs_weight, span_weight, span_of, tile_order, slab_start, resident
):
    leg = legendre.reshape(4, 8, SLOTS, TILE).transpose(0, 2, 1, 3)
    given = (
        leg,
        longitude,
        obs_weight.reshape(4, TILE),
        span_weight,
        span_of.reshape(4, TILE),
        tile_order,
        slab_start,
    )
    if len(SIZES) > 1:
        reached = (tile_order >= slab_start) & (tile_order < TILES)
        counts = jnp.sum(reached.reshape(SLOTS, NROW).astype(jnp.int32), axis=0)
        level = jnp.max(sum((counts > size).astype(jnp.int32) for size in SIZES[:-1]))
        product = lax.switch(level, [product_of(size, i) for i, size in enumerate(SIZES)], *given)
    else:
        product = product_of(SIZES[0], 0)(*given)
    return resident + product.reshape(resident.shape)


def solution(mesh):
    torus = Mesh(
        mesh.devices.reshape(NX, NYL, NCORE, NZ, NYH), ("x", "yl", "core", "z", "yh")
    )
    rows, cols = ("x", "yl", "core"), ("z", "yh")
    return jax.shard_map(
        per_device,
        mesh=torus,
        in_specs=(
            P(None, cols, None, rows, None),
            P(),
            P(),
            P(),
            P(),
            P(),
            P(),
            P(None, rows, cols, None, None),
        ),
        out_specs=P(None, rows, cols, None, None),
        check_vma=False,
    )
```
